32 devices in a mesh: gz: 4 (over y, core), xy: 8 (over z, x).
Axes of the slice: x: 2, y: 2, z: 4, core: 2. Of those that a mesh axis runs over, the one named last changes fastest.
Arguments:
- source: float32 [128, 32, 1024], P(('gz', 'xy')), may hold values from -10 to 11
- porosity: bfloat16 [128, 32, 1024], P(('gz', 'xy')), may hold values from 0.29882812 to 0.69921875
- concentration: bfloat16 [4, 128, 32, 1024], P(None, ('gz', 'xy')), may hold values from 0 to 1
- attachment: float32 [4], replicated, may hold values from 0.2 to 1
- neighbours: int32 [6, 128], P(None, ('gz', 'xy')), may hold values from -2 to 11, as said below
- position: int32 [128], P(('gz', 'xy')), may hold values from 0 to 3, as said below
- live: int32 [128], P(('gz', 'xy')), may hold values from 0 to 1, as said below
- inflow: float32 [16, 1024], P('xy'), may hold values from -8 to 8
Outputs:
- correction: float32 [128, 32, 1024], P(('gz', 'xy'))
- residual_rms: float32 [], replicated
The draws below stay inside these ranges and needn't reach their ends.
Inputs may be any that keep to these rules, and one draw needn't show every extreme that they name: Within each device the 4 slots hold the 4 positions of the device's block once each; position p is the brick at x brick p % 2 and streamwise layer p // 2 of the block. A slot with live 0 has every neighbour entry -1 and no entry names it. neighbours[f, b] names the live brick adjacent in space across face f of slot b: k in 0 to 3 is slot k of the same device; 4 + k is slot k of the previous device along gz for faces 0 and 1, along xy for faces 2 and 3; 8 + k the next device likewise. Across x faces neighbours are always on the same device; a streamwise neighbour on another device has the same x brick and lies in that device's last (face 0) or first (face 1) layer; a y neighbour has the same position. -1 marks an empty adjacent slot or the cross-section's edge, -2 the lower face of live bricks in the window's first layer and the upper face of those in its last layer. The relation is symmetric.
All inputs are finite; a program needn't handle non-finite values.
Results may differ from the reference program's by a relative error of at most 0.0004.
Values sent between devices are 32-bit elements; how exact they have to be, the bound alone decides.
A program may use at most 64 MiB of HBM per device.

```python
import math
import jax
import jax.numpy as jnp
from jax import lax

BRICK = 32
WX = 2
BZ = 2
CLASSES = 4
SWEEPS = 3
PLANE = 1024
SLOTS = 4
BRICKS = 128
XROWS = 16
N_GZ = 4
N_XY = 8


def brick_layout(key):
    devices = N_GZ * N_XY
    layout_key = jax.random.fold_in(key, 11)
    device_keys = jax.random.split(jax.random.fold_in(layout_key, 1), devices)
    slot_position = jax.vmap(lambda one_key: jax.random.permutation(one_key, SLOTS))(device_keys).astype(jnp.int32)
    pore_quota = jax.random.randint(jax.random.fold_in(layout_key, 2), (devices, 1), 4, 9)
    dice_rolls = jax.random.randint(jax.random.fold_in(layout_key, 3), (devices, SLOTS), 0, 8)
    live_at = (dice_rolls < pore_quota).astype(jnp.int32)
    slot_ids = jnp.arange(SLOTS, dtype=jnp.int32)
    slot_at = jnp.sum(jnp.where(slot_position[:, None, :] == slot_ids[None, :, None], slot_ids[None, None, :], 0), axis=2).astype(jnp.int32)
    live_slot = jnp.take_along_axis(live_at, slot_position, axis=1)
    device = jnp.broadcast_to(jnp.arange(devices, dtype=jnp.int32)[:, None], (devices, SLOTS))
    row_z = device // N_XY
    row_xy = device % N_XY
    column_x = slot_position % WX
    layer_index = slot_position // WX

    def lookup(target_device, target_position, offset, exists, boundary):
        safe_device = jnp.clip(target_device, 0, devices - 1)
        safe_position = jnp.clip(target_position, 0, SLOTS - 1)
        target_slot = slot_at[safe_device, safe_position]
        target_live = live_at[safe_device, safe_position]
        target_code = jnp.where(exists & (target_live == 1), offset + target_slot, -1)
        target_code = jnp.where(boundary, -2, target_code)
        return jnp.where(live_slot == 1, target_code, -1).astype(jnp.int32)
    inside_low = layer_index > 0
    inside_high = layer_index < BZ - 1
    lower_z = lookup(jnp.where(inside_low, device, device - N_XY), jnp.where(inside_low, slot_position - WX, column_x + (BZ - 1) * WX), jnp.where(inside_low, 0, SLOTS), inside_low | (row_z > 0), ~inside_low & (row_z == 0))
    upper_z = lookup(jnp.where(inside_high, device, device + N_XY), jnp.where(inside_high, slot_position + WX, column_x), jnp.where(inside_high, 0, 2 * SLOTS), inside_high | (row_z < N_GZ - 1), ~inside_high & (row_z == N_GZ - 1))
    never = jnp.zeros((devices, SLOTS), dtype=bool)
    lower_y = lookup(device - 1, slot_position, SLOTS, row_xy > 0, never)
    upper_y = lookup(device + 1, slot_position, 2 * SLOTS, row_xy < N_XY - 1, never)
    lower_x = lookup(device, slot_position - 1, 0, column_x > 0, never)
    upper_x = lookup(device, slot_position + 1, 0, column_x < WX - 1, never)
    table = jnp.stack([lower_z, upper_z, lower_y, upper_y, lower_x, upper_x]).reshape(6, devices * SLOTS)
    return (table, slot_position.reshape(-1), live_slot.reshape(-1).astype(jnp.int32))


def draw_neighbours(key, part):
    return brick_layout(key)[0]


def draw_position(key, part):
    return brick_layout(key)[1]


def draw_live(key, part):
    return brick_layout(key)[2]


def draw_source(key, part):
    full_shape = (BRICKS, BRICK, BRICK * BRICK)
    rising = (0.5 * 3.0 ** (jnp.arange(BRICKS, dtype=jnp.float32) / max(BRICKS - 1, 1)))[:, None, None]
    return jnp.clip(jax.random.normal(key, full_shape, jnp.float32), -6.0, 6.0) * rising


def block_levels(key, extent, cuts, smallest, largest):
    loudness, own = 1.0, jax.random.fold_in(key, 6)
    for axis_at, shards_of in cuts:
        heights = jnp.exp(jax.random.uniform(jax.random.fold_in(own, axis_at), (shards_of,), jnp.float32, smallest / len(cuts), largest / len(cuts)))
        loudness = loudness * jnp.repeat(heights, extent[axis_at] // shards_of).reshape([-1 if axis == axis_at else 1 for axis in range(len(extent))])
    return loudness


def gaussian(key, shape, deviation, reach, cuts=(), kind=jnp.bfloat16):
    values = jax.random.normal(key, shape, jnp.float32) * deviation
    if len(cuts) > 0:
        values = block_levels(key, shape, cuts, -0.22, 0.18) * values
    return jnp.clip(values, min=-reach, max=reach).astype(kind)


def setup_inputs(seed: int = 0) -> dict:
    streams_of = jax.random.split(jax.random.key(seed), 9)
    source = draw_source(jax.random.fold_in(streams_of[8], 71), 0)
    porosity = jnp.clip(0.29882812 + 0.40039062 * jax.random.uniform(streams_of[1], (BRICKS, BRICK, PLANE), jnp.float32) ** block_levels(streams_of[1], (BRICKS, BRICK, PLANE), ((0, 32),), -0.2, 0.2), 0.29882812, 0.69921875).astype(jnp.bfloat16)
    concentration = jnp.clip(1.0 * jax.random.uniform(streams_of[2], (CLASSES, BRICKS, BRICK, PLANE), jnp.float32) ** block_levels(streams_of[2], (CLASSES, BRICKS, BRICK, PLANE), ((1, 32),), -0.2, 0.2), 0.0, 1.0).astype(jnp.bfloat16)
    attachment = jnp.clip(jnp.exp(jax.random.uniform(streams_of[3], (CLASSES,), jnp.float32, math.log(0.2), math.log(1.0))), 0.2, 1.0)
    neighbours = draw_neighbours(jax.random.fold_in(streams_of[8], 71), 0)
    position = draw_position(jax.random.fold_in(streams_of[8], 71), 0)
    live = draw_live(jax.random.fold_in(streams_of[8], 71), 0)
    inflow = gaussian(streams_of[7], (XROWS, PLANE), 2.0, 8.0, ((0, 8),), jnp.float32)
    return {"source": source, "porosity": porosity, "concentration": concentration, "attachment": attachment, "neighbours": neighbours, "position": position, "live": live, "inflow": inflow}


SIGMA = 0.25
EPSILON = 1e-06

def face_of(field, face_side):
    brick_count, edge_cells, plane_cells = field.shape
    blocked = field.reshape(brick_count, edge_cells, edge_cells, edge_cells)
    if face_side == 0:
        surface = blocked[:, 0]
    elif face_side == 1:
        surface = blocked[:, edge_cells - 1]
    elif face_side == 2:
        surface = blocked[:, :, 0, :]
    elif face_side == 3:
        surface = blocked[:, :, edge_cells - 1, :]
    elif face_side == 4:
        surface = blocked[:, :, :, 0]
    else:
        surface = blocked[:, :, :, edge_cells - 1]
    return surface.reshape(brick_count, plane_cells)

def boundary_masks(edge_cells, plane_cells):
    layer_index = lax.broadcasted_iota(jnp.int32, (1, edge_cells, plane_cells), 1)
    column = lax.broadcasted_iota(jnp.int32, (1, edge_cells, plane_cells), 2)
    row_y = column // edge_cells
    column_x = column % edge_cells
    last_cell = edge_cells - 1
    return (layer_index == 0, layer_index == last_cell, row_y == 0, row_y == last_cell, column_x == 0, column_x == last_cell)

def neighbour_values(field, ghosts):
    brick_count, edge_cells, plane_cells = field.shape
    column = lax.broadcasted_iota(jnp.int32, (1, 1, plane_cells), 2) % edge_cells
    lower_z = jnp.concatenate([ghosts[0][:, None, :], field[:, :-1]], axis=1)
    upper_z = jnp.concatenate([field[:, 1:], ghosts[1][:, None, :]], axis=1)
    lower_y = jnp.concatenate([ghosts[2].reshape(brick_count, edge_cells, edge_cells), field[:, :, :-edge_cells]], axis=2)
    upper_y = jnp.concatenate([field[:, :, edge_cells:], ghosts[3].reshape(brick_count, edge_cells, edge_cells)], axis=2)
    lower_x = jnp.where(column == 0, jnp.repeat(ghosts[4].reshape(brick_count, edge_cells, edge_cells), edge_cells, axis=2), jnp.concatenate([field[:, :, :1], field[:, :, :-1]], axis=2))
    upper_x = jnp.where(column == edge_cells - 1, jnp.repeat(ghosts[5].reshape(brick_count, edge_cells, edge_cells), edge_cells, axis=2), jnp.concatenate([field[:, :, 1:], field[:, :, -1:]], axis=2))
    return (lower_z, upper_z, lower_y, upper_y, lower_x, upper_x)

def mobility_of(porosity, concentration, attachment, alive_mask):
    deposit = attachment[0] * concentration[0].astype(jnp.float32)
    for class_index in range(1, concentration.shape[0]):
        deposit = deposit + attachment[class_index] * concentration[class_index].astype(jnp.float32)
    pore_share = porosity.astype(jnp.float32)
    solid_share = 1.0 - pore_share
    swelling = 1.0 + deposit
    return alive_mask * (pore_share * pore_share * pore_share) / (solid_share * solid_share * swelling * swelling)

def coefficients(mobility, mobility_ghosts, open_faces):
    brick_count, edge_cells, plane_cells = mobility.shape
    beside = neighbour_values(mobility, mobility_ghosts)
    borders = boundary_masks(edge_cells, plane_cells)
    result = []
    for face_side in range(6):
        opening = jnp.where(borders[face_side], open_faces[face_side][:, None, None], 1.0)
        result.append(0.5 * (mobility + beside[face_side]) * opening)
    return result

def diagonal_of(coeffs):
    total_sum = SIGMA + coeffs[0]
    for face_side in range(1, 6):
        total_sum = total_sum + coeffs[face_side]
    return total_sum

def right_side_of(coeffs, source, alive_mask, inlet_values, inlet_flag):
    borders = boundary_masks(source.shape[1], source.shape[2])
    inlet_term = jnp.where(borders[0] & inlet_flag[:, None, None], coeffs[0] * inlet_values[:, None, :], 0.0)
    return alive_mask * source + inlet_term

def apply_operator(field, ghosts, coeffs):
    beside = neighbour_values(field, ghosts)
    operated = SIGMA * field
    for face_side in range(6):
        operated = operated + coeffs[face_side] * (field - beside[face_side])
    return operated

def global_neighbours(neighbours):
    brick_index = jnp.arange(neighbours.shape[1], dtype=jnp.int32)
    device = brick_index // SLOTS
    offsets = (-N_XY, N_XY, -1, 1, 0, 0)
    result = []
    for face_side in range(6):
        local_code = neighbours[face_side]
        slot_index = local_code % SLOTS
        moved_device = jnp.where(local_code >= SLOTS, device + offsets[face_side], device)
        result.append(jnp.where(local_code >= 0, moved_device * SLOTS + slot_index, local_code))
    return jnp.stack(result)

def ghost_faces(field, global_index, keep_own):
    result = []
    for face_side in range(6):
        other_side = face_of(field, face_side ^ 1)
        target = global_index[face_side]
        picked = jnp.take(other_side, jnp.clip(target, 0, field.shape[0] - 1), axis=0)
        fallback = face_of(field, face_side) if keep_own else jnp.zeros_like(picked)
        result.append(jnp.where((target >= 0)[:, None], picked, jnp.where((target == -2)[:, None], fallback, jnp.zeros_like(picked))))
    return jnp.stack(result)

def to_blocks(array, devices):
    return array.reshape((devices, array.shape[0] // devices) + array.shape[1:])

def stacked_blocks(array, devices):
    return jnp.swapaxes(array.reshape((array.shape[0], devices, array.shape[1] // devices) + array.shape[2:]), 0, 1)

def reference(source, porosity, concentration, attachment, neighbours, position, live, inflow):
    total_bricks, edge_cells, plane_cells = source.shape
    devices = total_bricks // SLOTS
    alive_mask = live.astype(jnp.float32)[:, None, None]
    mobility = mobility_of(porosity, concentration, attachment, alive_mask)
    global_index = global_neighbours(neighbours)
    open_faces = (global_index != -1).astype(jnp.float32)
    mobility_ghosts = ghost_faces(mobility, global_index, True)
    brick_index = jnp.arange(total_bricks, dtype=jnp.int32)
    inlet_rows = brick_index // SLOTS % N_XY * WX + position % WX
    inlet_values = jnp.take(inflow, inlet_rows, axis=0)
    inlet_flag = global_index[0] == -2
    mobility_blocks = to_blocks(mobility, devices)
    mobility_ghost_blocks = stacked_blocks(mobility_ghosts, devices)
    open_blocks = stacked_blocks(open_faces, devices)

    def prepare(pieces):
        block_mobility, block_ghosts, block_open, block_source, block_alive, block_inlet, block_flag = pieces
        coeffs = coefficients(block_mobility, block_ghosts, block_open)
        return (diagonal_of(coeffs), right_side_of(coeffs, block_source, block_alive, block_inlet, block_flag))
    diagonal, right_side = lax.map(prepare, (mobility_blocks, mobility_ghost_blocks, open_blocks, to_blocks(source, devices), to_blocks(alive_mask, devices), to_blocks(inlet_values, devices), to_blocks(inlet_flag, devices)))
    diagonal = diagonal.reshape(source.shape)
    right_side = right_side.reshape(source.shape)

    def operate_block(pieces):
        block_field, block_ghosts, block_mobility, block_mobility_ghosts, block_open = pieces
        coeffs = coefficients(block_mobility, block_mobility_ghosts, block_open)
        return apply_operator(block_field, block_ghosts, coeffs)
    solution = jnp.zeros(source.shape, jnp.float32)
    residual = right_side
    for sweep_index in range(SWEEPS):
        precond = residual / diagonal
        ghosts = ghost_faces(precond, global_index, False)
        operated = lax.map(operate_block, (to_blocks(precond, devices), stacked_blocks(ghosts, devices), mobility_blocks, mobility_ghost_blocks, open_blocks)).reshape(source.shape)
        inner_rw = jnp.sum(residual * operated)
        inner_ww = jnp.sum(operated * operated)
        step_size = inner_rw / (inner_ww + EPSILON)
        solution = solution + step_size * precond
        residual = residual - step_size * operated
    squares = jnp.sum(residual * residual)
    residual_rms = jnp.sqrt(squares / float(total_bricks * edge_cells * plane_cells) + EPSILON)
    return (solution, residual_rms)
```

```python
import functools

import jax
import jax.numpy as jnp
from jax import lax
from jax.experimental import pallas as pl
from jax.experimental.pallas import tpu as pltpu
from jax.sharding import PartitionSpec as P

MESH = pl.DeviceIdType.MESH
SIGMA = 0.25
EPSILON = 1e-06
EDGE = 32
LANES = 128
BLOCKS = 8
BASE = 8
DEPTH = 64
PAIRS = [(i, j) for j in range(4) for i in range(j + 1)]


def kernel(
    n_gz, n_xy,
    position, live, attachment,
    source, porosity, concentration, inflow,
    out, rms,
    src_v, por_v, con_v,
    mob, pk, coef, inv, uk,
    zsend, zrecv, ysend, yrecv, gsum, gslot, xsum, xslot,
    load_sem, send_sem, recv_sem, gsend_sem, grecv_sem, xsend_sem, xrecv_sem,
):
    gz, xy = lax.axis_index("gz"), lax.axis_index("xy")
    loads = [
        pltpu.make_async_copy(porosity, por_v, load_sem.at[0]),
        pltpu.make_async_copy(concentration, con_v, load_sem.at[1]),
        pltpu.make_async_copy(source, src_v, load_sem.at[2]),
    ]
    for load in loads:
        load.start()

    barrier = pltpu.get_barrier_semaphore()
    for o in range(1, n_gz):
        pl.semaphore_signal(barrier, inc=1, device_id={"gz": lax.rem(gz + o, n_gz)}, device_id_type=MESH)
    for o in range(1, n_xy):
        pl.semaphore_signal(barrier, inc=1, device_id={"xy": lax.rem(xy + o, n_xy)}, device_id_type=MESH)

    spots = [jnp.full((EDGE, LANES), position[b], jnp.int32) for b in range(4)]
    alive = [live[b].astype(jnp.float32) for b in range(4)]

    def pick(chunks, keys):
        result = chunks[0]
        for chunk, key in zip(chunks[1:], keys[1:]):
            result = jnp.where(key, chunk, result)
        return result

    lane = lax.broadcasted_iota(jnp.int32, (EDGE, LANES), 1)
    group = lane // EDGE
    low_group, high_group = group == 0, group == 3
    low_x, high_x = lane % EDGE == 0, lane % EDGE == EDGE - 1
    row = lax.broadcasted_iota(jnp.int32, (EDGE, LANES), 0)

    def rows(zl):
        return pl.ds(BASE + zl * EDGE, EDGE)

    for load in loads:
        load.wait()

    def mobility_step(i, _):
        cols = pl.ds(pl.multiple_of(i * LANES, LANES), LANES)
        found, right = [], []
        for slot in range(4):
            deposit = attachment[0] * con_v[0, slot, :, cols].astype(jnp.float32)
            for c in range(1, 4):
                deposit = deposit + attachment[c] * con_v[c, slot, :, cols].astype(jnp.float32)
            pore = por_v[slot, :, cols].astype(jnp.float32)
            dense = (1.0 - pore) * (1.0 + deposit)
            found.append(alive[slot] * (pore * pore * pore) / (dense * dense))
            right.append(alive[slot] * src_v[slot, :, cols])
        for q in range(4):
            keys = [spot == q for spot in spots]
            mob[q % 2, i + 1, rows(q // 2), :] = pick(found, keys)
            uk[0, q % 2, i, q // 2] = pick(right, keys)
        return 0

    lax.fori_loop(0, BLOCKS, mobility_step, 0)

    sources = (gz > 0, gz < n_gz - 1, xy > 0, xy < n_xy - 1)
    targets = (sources[1], sources[0], sources[3], sources[2])
    ids = ({"gz": gz + 1}, {"gz": gz - 1}, {"xy": xy + 1}, {"xy": xy - 1})

    def face_copy(e, d):
        send, recv = (zsend, zrecv) if d < 2 else (ysend, yrecv)
        return pltpu.make_async_remote_copy(
            src_ref=send.at[e, d % 2], dst_ref=recv.at[e, d % 2],
            send_sem=send_sem.at[e, d], recv_sem=recv_sem.at[e, d],
            device_id=ids[d], device_id_type=MESH,
        )

    def send_faces(ref, e, keep_own):
        for k, last in ((0, BASE + DEPTH - 1), (1, BASE)):
            for xb in range(2):
                for i in range(BLOCKS):
                    at = xb * BLOCKS + i
                    zsend[e, k, at:at + 1, :] = ref[xb, i + 1, last:last + 1, :]
        for k, (block, shift) in enumerate(((BLOCKS, 32), (1, 0))):
            packed = None
            for j in range(4):
                chunk = ref[j % 2, block, rows(j // 2), :]
                turn = (EDGE * j + shift) % LANES
                chunk = pltpu.roll(chunk, turn, 1) if turn else chunk
                packed = chunk if packed is None else jnp.where(group == j, chunk, packed)
            ysend[e, k] = packed
        if e == 0:
            pl.semaphore_wait(barrier, n_gz + n_xy - 2)
        for d in (2, 3, 0, 1):
            @pl.when(targets[d])
            def _(d=d):
                face_copy(e, d).start()
        for d in range(4):
            @pl.when(jnp.logical_not(sources[d]))
            def _(d=d):
                if d < 2:
                    zrecv[e, d] = zsend[e, 1 - d] if keep_own else jnp.zeros((16, LANES), jnp.float32)
                else:
                    yrecv[e, d - 2] = jnp.zeros((EDGE, LANES), jnp.float32)

    def take_faces(ref, e):
        for d in (0, 1):
            @pl.when(sources[d])
            def _(d=d):
                face_copy(e, d).wait_recv()
            at_row = BASE - 1 if d == 0 else BASE + DEPTH
            for xb in range(2):
                for i in range(BLOCKS):
                    at = xb * BLOCKS + i
                    ref[xb, i + 1, at_row:at_row + 1, :] = zrecv[e, d, at:at + 1, :]
        for d in (2, 3):
            @pl.when(sources[d])
            def _(d=d):
                face_copy(e, d).wait_recv()
            got = yrecv[e, d - 2]
            for j in range(4):
                turn = ((96 if d == 2 else 0) - EDGE * j) % LANES
                chunk = pltpu.roll(got, turn, 1) if turn else got
                ref[j % 2, 0 if d == 2 else BLOCKS + 1, rows(j // 2), :] = chunk

    def beside(ref, i, zl):
        r = BASE + zl * EDGE
        here = [ref[xb, i + 1, r:r + EDGE, :] for xb in range(2)]
        result = []
        for xb in range(2):
            v = here[xb]
            before, after = ref[xb, i, r:r + EDGE, :], ref[xb, i + 2, r:r + EDGE, :]
            lower_y = pltpu.roll(jnp.where(high_group, before, v), 32, 1)
            upper_y = pltpu.roll(jnp.where(low_group, after, v), 96, 1)
            lower_x, upper_x = pltpu.roll(v, 1, 1), pltpu.roll(v, 127, 1)
            if xb == 1:
                lower_x = jnp.where(low_x, pltpu.roll(here[0], 97, 1), lower_x)
            else:
                upper_x = jnp.where(high_x, pltpu.roll(here[1], 31, 1), upper_x)
            result.append((
                ref[xb, i + 1, r - 1:r - 1 + EDGE, :], ref[xb, i + 1, r + 1:r + 1 + EDGE, :],
                lower_y, upper_y, lower_x, upper_x,
            ))
        return here, result

    def folded(x):
        return (x[0:8] + x[8:16]) + (x[16:24] + x[24:32])

    send_faces(mob, 0, True)
    take_faces(mob, 0)
    first = jnp.where(gz == 0, 1.0, 0.0)

    def coefficient_step(i, total):
        cols = pl.ds(pl.multiple_of(i * LANES, LANES), LANES)
        for zl in range(2):
            here, near = beside(mob, i, zl)
            for xb in range(2):
                m = here[xb]
                diagonal = SIGMA
                inlet = None
                for f in range(6):
                    other = near[xb][f]
                    c = jnp.where(jnp.minimum(m, other) > 0.0, 0.5 * (m + other), 0.0)
                    if f == 4 and xb == 0:
                        c = jnp.where(low_x, 0.0, c)
                    if f == 5 and xb == 1:
                        c = jnp.where(high_x, 0.0, c)
                    coef[f, xb, i, zl] = c
                    diagonal = diagonal + c
                    inlet = c if f == 0 else inlet
                b = uk[0, xb, i, zl]
                if zl == 0:
                    b = b + jnp.where(row == 0, first * inlet * inflow[xb:xb + 1, cols], 0.0)
                inverse = 1.0 / diagonal
                inv[xb, i, zl] = inverse
                uk[0, xb, i, zl] = b
                pk[0, xb, i + 1, rows(zl), :] = b * inverse
                total = total + folded(b * b)
        return total

    zero = jnp.zeros((8, LANES), jnp.float32)
    grams = [lax.fori_loop(0, BLOCKS, coefficient_step, zero)]

    for k in range(3):
        send_faces(pk.at[k], k + 1, False)
        take_faces(pk.at[k], k + 1)

        def sweep_step(i, totals, k=k):
            totals = list(totals)
            for zl in range(2):
                here, near = beside(pk.at[k], i, zl)
                for xb in range(2):
                    u = uk[k, xb, i, zl]
                    away = coef[0, xb, i, zl] * near[xb][0]
                    for f in range(1, 6):
                        away = away + coef[f, xb, i, zl] * near[xb][f]
                    new = u - away
                    if k < 2:
                        uk[k + 1, xb, i, zl] = new
                        pk[k + 1, xb, i + 1, rows(zl), :] = new * inv[xb, i, zl]
                    for j in range(k + 2):
                        left = new if j == k + 1 else u if j == k else uk[j, xb, i, zl]
                        totals[j] = totals[j] + folded(left * new)
            return tuple(totals)

        grams.extend(lax.fori_loop(0, BLOCKS, sweep_step, (zero,) * (k + 2)))

    parts = [jnp.sum(g, axis=0, keepdims=True) for g in grams]
    for at, part in enumerate(parts):
        gsum[at:at + 1, :] = part
    gsum[len(parts):, :] = jnp.zeros((16 - len(parts), LANES), jnp.float32)

    def gather(total, slot, send, recv, axis, me, n):
        copies = []
        for o in range(1, n):
            copies.append(pltpu.make_async_remote_copy(
                src_ref=total, dst_ref=slot.at[me], send_sem=send.at[o], recv_sem=recv.at[o],
                device_id={axis: lax.rem(me + o, n)}, device_id_type=MESH,
            ))
            copies[-1].start()
        slot[me] = total[...]
        for copy in copies:
            copy.wait_recv()
        result = slot[0]
        for s in range(1, n):
            result = result + slot[s]
        return copies, result

    gz_copies, result = gather(gsum, gslot, gsend_sem, grecv_sem, "gz", gz, n_gz)
    xsum[...] = result
    xy_copies, result = gather(xsum, xslot, xsend_sem, xrecv_sem, "xy", xy, n_xy)
    result = jnp.broadcast_to(jnp.sum(result, axis=1, keepdims=True), (16, LANES))
    g = {}
    for at, (i, j) in enumerate(PAIRS):
        g[i, j] = g[j, i] = result[at:at + 1, :]

    s0 = g[0, 1] / (g[1, 1] + EPSILON)
    rw = g[0, 1] - s0 * (g[0, 2] + g[1, 1]) + s0 * s0 * g[1, 2]
    ww = g[1, 1] - 2.0 * s0 * g[1, 2] + s0 * s0 * g[2, 2]
    s1 = rw / (ww + EPSILON)
    a = (jnp.ones_like(s0), -(s0 + s1), s0 * s1)

    def form(di, dj):
        total = 0.0
        for i in range(3):
            for j in range(3):
                total = total + a[i] * a[j] * g[i + di, j + dj]
        return total

    rr, rw, ww = form(0, 0), form(0, 1), form(1, 1)
    s2 = rw / (ww + EPSILON)
    squares = rr - 2.0 * s2 * rw + s2 * s2 * ww
    voxels = float(4 * EDGE * EDGE * EDGE * n_gz * n_xy)
    rms[...] = jnp.sqrt(jnp.maximum(squares, 0.0) / voxels + EPSILON)
    w0 = s0 + s1 + s2
    w1 = s2 * a[1] - s0 * s1
    w2 = s2 * a[2]

    def output_step(i, _):
        cols = pl.ds(pl.multiple_of(i * LANES, LANES), LANES)
        found = []
        for q in range(4):
            xb, at = q % 2, rows(q // 2)
            found.append(
                w0 * pk[0, xb, i + 1, at, :] + w1 * pk[1, xb, i + 1, at, :] + w2 * pk[2, xb, i + 1, at, :]
            )
        for slot in range(4):
            out[slot, :, cols] = pick(found, [spots[slot] == q for q in range(4)])
        return 0

    lax.fori_loop(0, BLOCKS, output_step, 0)

    for e in range(4):
        for d in range(4):
            @pl.when(targets[d])
            def _(e=e, d=d):
                face_copy(e, d).wait_send()
    for copy in gz_copies + xy_copies:
        copy.wait_send()


def solution(mesh):
    n_gz, n_xy = mesh.shape["gz"], mesh.shape["xy"]

    def per_device(source, porosity, concentration, attachment, neighbours, position, live, inflow):
        f32 = jnp.float32
        smem = pl.BlockSpec(memory_space=pltpu.SMEM)
        vmem = pl.BlockSpec(memory_space=pltpu.VMEM)
        hbm = pl.BlockSpec(memory_space=pl.ANY)
        padded = (2, BLOCKS + 2, BASE + DEPTH + 8, LANES)
        plain = (2, BLOCKS, 2, EDGE, LANES)
        dma = pltpu.SemaphoreType.DMA
        out, rms = pl.pallas_call(
            functools.partial(kernel, n_gz, n_xy),
            out_shape=(
                jax.ShapeDtypeStruct(source.shape, f32),
                jax.ShapeDtypeStruct((1, LANES), f32),
            ),
            in_specs=[smem, smem, smem, hbm, hbm, hbm, vmem],
            out_specs=(vmem, vmem),
            scratch_shapes=[
                pltpu.VMEM(source.shape, f32),
                pltpu.VMEM(porosity.shape, porosity.dtype),
                pltpu.VMEM(concentration.shape, concentration.dtype),
                pltpu.VMEM(padded, f32),
                pltpu.VMEM((3,) + padded, f32),
                pltpu.VMEM((6,) + plain, f32),
                pltpu.VMEM(plain, f32),
                pltpu.VMEM((3,) + plain, f32),
                pltpu.VMEM((4, 2, 16, LANES), f32),
                pltpu.VMEM((4, 2, 16, LANES), f32),
                pltpu.VMEM((4, 2, EDGE, LANES), f32),
                pltpu.VMEM((4, 2, EDGE, LANES), f32),
                pltpu.VMEM((16, LANES), f32),
                pltpu.VMEM((n_gz, 16, LANES), f32),
                pltpu.VMEM((16, LANES), f32),
                pltpu.VMEM((n_xy, 16, LANES), f32),
                dma((3,)),
                dma((4, 4)),
                dma((4, 4)),
                dma((n_gz,)),
                dma((n_gz,)),
                dma((n_xy,)),
                dma((n_xy,)),
            ],
            compiler_params=pltpu.CompilerParams(
                collective_id=0, has_side_effects=True, vmem_limit_bytes=48 << 20
            ),
        )(position, live, attachment, source, porosity, concentration, inflow)
        return out, rms[0, 0]

    spread = ("gz", "xy")
    in_specs = (
        P(spread, None, None), P(spread, None, None), P(None, spread, None, None), P(),
        P(None, spread), P(spread), P(spread), P("xy", None),
    )
    return jax.shard_map(
        per_device, mesh=mesh, in_specs=in_specs,
        out_specs=(P(spread, None, None), P()), check_vma=False,
    )
```

```python
import functools

import jax
import jax.numpy as jnp
from jax import lax
from jax.experimental import pallas as pl
from jax.experimental.pallas import tpu as pltpu
from jax.sharding import PartitionSpec as P

MESH = pl.DeviceIdType.MESH
SIGMA = 0.25
EPSILON = 1e-06
EDGE = 32
LANES = 128
BLOCKS = 8
BASE = 8
DEPTH = 64
PAIRS = [(i, j) for j in range(4) for i in range(j + 1)]


def kernel(
    n_gz, n_xy,
    position_hbm, live_hbm, attachment_hbm,
    source, porosity, concentration, inflow_hbm,
    out, rms,
    position, live, attachment, inflow,
    src_v, por_v, con_v,
    mob, pk, coef, inv, uk,
    zsend, zrecv, ysend, yrecv, gsum, gslot, xsum, xslot,
    load_sem, send_sem, recv_sem, gsend_sem, grecv_sem, xsend_sem, xrecv_sem,
):
    gz, xy = lax.axis_index("gz"), lax.axis_index("xy")
    loads = [
        pltpu.make_async_copy(porosity, por_v, load_sem.at[0]),
        pltpu.make_async_copy(concentration, con_v, load_sem.at[1]),
        pltpu.make_async_copy(source, src_v, load_sem.at[2]),
        pltpu.make_async_copy(inflow_hbm, inflow, load_sem.at[3]),
        pltpu.make_async_copy(position_hbm, position, load_sem.at[4]),
        pltpu.make_async_copy(live_hbm, live, load_sem.at[5]),
        pltpu.make_async_copy(attachment_hbm, attachment, load_sem.at[6]),
    ]
    for load in loads:
        load.start()

    barrier = pltpu.get_barrier_semaphore()
    for o in range(1, n_gz):
        pl.semaphore_signal(barrier, inc=1, device_id={"gz": lax.rem(gz + o, n_gz)}, device_id_type=MESH)
    for o in range(1, n_xy):
        pl.semaphore_signal(barrier, inc=1, device_id={"xy": lax.rem(xy + o, n_xy)}, device_id_type=MESH)

    for load in loads:
        load.wait()
    spots = [jnp.full((EDGE, LANES), position[b], jnp.int32) for b in range(4)]
    alive = [live[b].astype(jnp.float32) for b in range(4)]

    def pick(chunks, keys):
        result = chunks[0]
        for chunk, key in zip(chunks[1:], keys[1:]):
            result = jnp.where(key, chunk, result)
        return result

    lane = lax.broadcasted_iota(jnp.int32, (EDGE, LANES), 1)
    group = lane // EDGE
    low_group, high_group = group == 0, group == 3
    low_x, high_x = lane % EDGE == 0, lane % EDGE == EDGE - 1
    row = lax.broadcasted_iota(jnp.int32, (EDGE, LANES), 0)

    def rows(zl):
        return pl.ds(BASE + zl * EDGE, EDGE)


    def mobility_step(i, _):
        cols = pl.ds(pl.multiple_of(i * LANES, LANES), LANES)
        found, right = [], []
        for slot in range(4):
            deposit = attachment[0] * con_v[0, slot, :, cols].astype(jnp.float32)
            for c in range(1, 4):
                deposit = deposit + attachment[c] * con_v[c, slot, :, cols].astype(jnp.float32)
            pore = por_v[slot, :, cols].astype(jnp.float32)
            dense = (1.0 - pore) * (1.0 + deposit)
            found.append(alive[slot] * (pore * pore * pore) / (dense * dense))
            right.append(alive[slot] * src_v[slot, :, cols])
        for q in range(4):
            keys = [spot == q for spot in spots]
            mob[q % 2, i + 1, rows(q // 2), :] = pick(found, keys)
            uk[0, q % 2, i, q // 2] = pick(right, keys)
        return 0

    lax.fori_loop(0, BLOCKS, mobility_step, 0)

    sources = (gz > 0, gz < n_gz - 1, xy > 0, xy < n_xy - 1)
    targets = (sources[1], sources[0], sources[3], sources[2])
    ids = ({"gz": gz + 1}, {"gz": gz - 1}, {"xy": xy + 1}, {"xy": xy - 1})

    def face_copy(e, d):
        send, recv = (zsend, zrecv) if d < 2 else (ysend, yrecv)
        return pltpu.make_async_remote_copy(
            src_ref=send.at[e, d % 2], dst_ref=recv.at[e, d % 2],
            send_sem=send_sem.at[e, d], recv_sem=recv_sem.at[e, d],
            device_id=ids[d], device_id_type=MESH,
        )

    def send_faces(ref, e, keep_own):
        for k, last in ((0, BASE + DEPTH - 1), (1, BASE)):
            for xb in range(2):
                for i in range(BLOCKS):
                    at = xb * BLOCKS + i
                    zsend[e, k, at:at + 1, :] = ref[xb, i + 1, last:last + 1, :]
        for k, (block, shift) in enumerate(((BLOCKS, 32), (1, 0))):
            packed = None
            for j in range(4):
                chunk = ref[j % 2, block, rows(j // 2), :]
                turn = (EDGE * j + shift) % LANES
                chunk = pltpu.roll(chunk, turn, 1) if turn else chunk
                packed = chunk if packed is None else jnp.where(group == j, chunk, packed)
            ysend[e, k] = packed
        if e == 0:
            pl.semaphore_wait(barrier, n_gz + n_xy - 2)
        for d in (2, 3, 0, 1):
            @pl.when(targets[d])
            def _(d=d):
                face_copy(e, d).start()
        for d in range(4):
            @pl.when(jnp.logical_not(sources[d]))
            def _(d=d):
                if d < 2:
                    zrecv[e, d] = zsend[e, 1 - d] if keep_own else jnp.zeros((16, LANES), jnp.float32)
                else:
                    yrecv[e, d - 2] = jnp.zeros((EDGE, LANES), jnp.float32)

    def take_z(ref, e):
        for d in (0, 1):
            @pl.when(sources[d])
            def _(d=d):
                face_copy(e, d).wait_recv()
            at_row = BASE - 1 if d == 0 else BASE + DEPTH
            for xb in range(2):
                for i in range(BLOCKS):
                    at = xb * BLOCKS + i
                    ref[xb, i + 1, at_row:at_row + 1, :] = zrecv[e, d, at:at + 1, :]

    def take_y(ref, e):
        for d in (2, 3):
            @pl.when(sources[d])
            def _(d=d):
                face_copy(e, d).wait_recv()
            got = yrecv[e, d - 2]
            for j in range(4):
                turn = ((96 if d == 2 else 0) - EDGE * j) % LANES
                chunk = pltpu.roll(got, turn, 1) if turn else got
                ref[j % 2, 0 if d == 2 else BLOCKS + 1, rows(j // 2), :] = chunk

    def beside(ref, i, zl):
        r = BASE + zl * EDGE
        here = [ref[xb, i + 1, r:r + EDGE, :] for xb in range(2)]
        result = []
        for xb in range(2):
            v = here[xb]
            before, after = ref[xb, i, r:r + EDGE, :], ref[xb, i + 2, r:r + EDGE, :]
            lower_y = pltpu.roll(jnp.where(high_group, before, v), 32, 1)
            upper_y = pltpu.roll(jnp.where(low_group, after, v), 96, 1)
            lower_x, upper_x = pltpu.roll(v, 1, 1), pltpu.roll(v, 127, 1)
            if xb == 1:
                lower_x = jnp.where(low_x, pltpu.roll(here[0], 97, 1), lower_x)
            else:
                upper_x = jnp.where(high_x, pltpu.roll(here[1], 31, 1), upper_x)
            result.append((
                ref[xb, i + 1, r - 1:r - 1 + EDGE, :], ref[xb, i + 1, r + 1:r + 1 + EDGE, :],
                lower_y, upper_y, lower_x, upper_x,
            ))
        return here, result

    def over_blocks(step, carry, ref, e):
        take_z(ref, e)
        carry = lax.fori_loop(1, BLOCKS - 1, step, carry)
        take_y(ref, e)
        return lax.fori_loop(0, 2, lambda j, c: step(j * (BLOCKS - 1), c), carry)

    def folded(x):
        return (x[0:8] + x[8:16]) + (x[16:24] + x[24:32])

    send_faces(mob, 0, True)
    first = jnp.where(gz == 0, 1.0, 0.0)

    def coefficient_step(i, total):
        cols = pl.ds(pl.multiple_of(i * LANES, LANES), LANES)
        for zl in range(2):
            here, near = beside(mob, i, zl)
            for xb in range(2):
                m = here[xb]
                diagonal = SIGMA
                inlet = None
                for f in range(6):
                    other = near[xb][f]
                    c = jnp.where(jnp.minimum(m, other) > 0.0, 0.5 * (m + other), 0.0)
                    if f == 4 and xb == 0:
                        c = jnp.where(low_x, 0.0, c)
                    if f == 5 and xb == 1:
                        c = jnp.where(high_x, 0.0, c)
                    coef[f, xb, i, zl] = c
                    diagonal = diagonal + c
                    inlet = c if f == 0 else inlet
                b = uk[0, xb, i, zl]
                if zl == 0:
                    b = b + jnp.where(row == 0, first * inlet * inflow[xb:xb + 1, cols], 0.0)
                inverse = 1.0 / diagonal
                inv[xb, i, zl] = inverse
                uk[0, xb, i, zl] = b
                pk[0, xb, i + 1, rows(zl), :] = b * inverse
                total = total + folded(b * b)
        return total

    zero = jnp.zeros((8, LANES), jnp.float32)
    grams = [over_blocks(coefficient_step, zero, mob, 0)]

    for k in range(3):
        send_faces(pk.at[k], k + 1, False)

        def sweep_step(i, totals, k=k):
            totals = list(totals)
            for zl in range(2):
                here, near = beside(pk.at[k], i, zl)
                for xb in range(2):
                    u = uk[k, xb, i, zl]
                    away = coef[0, xb, i, zl] * near[xb][0]
                    for f in range(1, 6):
                        away = away + coef[f, xb, i, zl] * near[xb][f]
                    new = u - away
                    if k < 2:
                        uk[k + 1, xb, i, zl] = new
                        pk[k + 1, xb, i + 1, rows(zl), :] = new * inv[xb, i, zl]
                    for j in range(k + 2):
                        left = new if j == k + 1 else u if j == k else uk[j, xb, i, zl]
                        totals[j] = totals[j] + folded(left * new)
            return tuple(totals)

        grams.extend(over_blocks(sweep_step, (zero,) * (k + 2), pk.at[k], k + 1))

    parts = [jnp.sum(g, axis=0, keepdims=True) for g in grams]
    for at, part in enumerate(parts):
        gsum[at:at + 1, :] = part
    gsum[len(parts):, :] = jnp.zeros((16 - len(parts), LANES), jnp.float32)

    def gather(total, slot, send, recv, axis, me, n):
        copies = []
        for o in range(1, n):
            copies.append(pltpu.make_async_remote_copy(
                src_ref=total, dst_ref=slot.at[me], send_sem=send.at[o], recv_sem=recv.at[o],
                device_id={axis: lax.rem(me + o, n)}, device_id_type=MESH,
            ))
            copies[-1].start()
        slot[me] = total[...]
        for copy in copies:
            copy.wait_recv()
        result = slot[0]
        for s in range(1, n):
            result = result + slot[s]
        return copies, result

    gz_copies, result = gather(gsum, gslot, gsend_sem, grecv_sem, "gz", gz, n_gz)
    xsum[...] = result
    xy_copies, result = gather(xsum, xslot, xsend_sem, xrecv_sem, "xy", xy, n_xy)
    result = jnp.broadcast_to(jnp.sum(result, axis=1, keepdims=True), (16, LANES))
    g = {}
    for at, (i, j) in enumerate(PAIRS):
        g[i, j] = g[j, i] = result[at:at + 1, :]

    s0 = g[0, 1] / (g[1, 1] + EPSILON)
    rw = g[0, 1] - s0 * (g[0, 2] + g[1, 1]) + s0 * s0 * g[1, 2]
    ww = g[1, 1] - 2.0 * s0 * g[1, 2] + s0 * s0 * g[2, 2]
    s1 = rw / (ww + EPSILON)
    a = (jnp.ones_like(s0), -(s0 + s1), s0 * s1)

    def form(di, dj):
        total = 0.0
        for i in range(3):
            for j in range(3):
                total = total + a[i] * a[j] * g[i + di, j + dj]
        return total

    rr, rw, ww = form(0, 0), form(0, 1), form(1, 1)
    s2 = rw / (ww + EPSILON)
    squares = rr - 2.0 * s2 * rw + s2 * s2 * ww
    voxels = float(4 * EDGE * EDGE * EDGE * n_gz * n_xy)
    rms[...] = jnp.sqrt(jnp.maximum(squares, 0.0) / voxels + EPSILON)
    w0 = s0 + s1 + s2
    w1 = s2 * a[1] - s0 * s1
    w2 = s2 * a[2]

    def output_step(i, _):
        cols = pl.ds(pl.multiple_of(i * LANES, LANES), LANES)
        found = []
        for q in range(4):
            xb, at = q % 2, rows(q // 2)
            found.append(
                w0 * pk[0, xb, i + 1, at, :] + w1 * pk[1, xb, i + 1, at, :] + w2 * pk[2, xb, i + 1, at, :]
            )
        for slot in range(4):
            out[slot, :, cols] = pick(found, [spots[slot] == q for q in range(4)])
        return 0

    lax.fori_loop(0, BLOCKS, output_step, 0)

    for e in range(4):
        for d in range(4):
            @pl.when(targets[d])
            def _(e=e, d=d):
                face_copy(e, d).wait_send()
    for copy in gz_copies + xy_copies:
        copy.wait_send()


def solution(mesh):
    n_gz, n_xy = mesh.shape["gz"], mesh.shape["xy"]

    def per_device(source, porosity, concentration, attachment, neighbours, position, live, inflow):
        f32 = jnp.float32
        vmem = pl.BlockSpec(memory_space=pltpu.VMEM)
        hbm = pl.BlockSpec(memory_space=pltpu.HBM)
        padded = (2, BLOCKS + 2, BASE + DEPTH + 8, LANES)
        plain = (2, BLOCKS, 2, EDGE, LANES)
        dma = pltpu.SemaphoreType.DMA
        out, rms = pl.pallas_call(
            functools.partial(kernel, n_gz, n_xy),
            out_shape=(
                jax.ShapeDtypeStruct(source.shape, f32),
                jax.ShapeDtypeStruct((1, LANES), f32),
            ),
            in_specs=[hbm] * 7,
            out_specs=(vmem, vmem),
            scratch_shapes=[
                pltpu.SMEM(position.shape, jnp.int32),
                pltpu.SMEM(live.shape, jnp.int32),
                pltpu.SMEM(attachment.shape, f32),
                pltpu.VMEM(inflow.shape, f32),
                pltpu.VMEM(source.shape, f32),
                pltpu.VMEM(porosity.shape, porosity.dtype),
                pltpu.VMEM(concentration.shape, concentration.dtype),
                pltpu.VMEM(padded, f32),
                pltpu.VMEM((3,) + padded, f32),
                pltpu.VMEM((6,) + plain, f32),
                pltpu.VMEM(plain, f32),
                pltpu.VMEM((3,) + plain, f32),
                pltpu.VMEM((4, 2, 16, LANES), f32),
                pltpu.VMEM((4, 2, 16, LANES), f32),
                pltpu.VMEM((4, 2, EDGE, LANES), f32),
                pltpu.VMEM((4, 2, EDGE, LANES), f32),
                pltpu.VMEM((16, LANES), f32),
                pltpu.VMEM((n_gz, 16, LANES), f32),
                pltpu.VMEM((16, LANES), f32),
                pltpu.VMEM((n_xy, 16, LANES), f32),
                dma((7,)),
                dma((4, 4)),
                dma((4, 4)),
                dma((n_gz,)),
                dma((n_gz,)),
                dma((n_xy,)),
                dma((n_xy,)),
            ],
            compiler_params=pltpu.CompilerParams(
                collective_id=0, has_side_effects=True, vmem_limit_bytes=66_000_000
            ),
        )(position, live, attachment, source, porosity, concentration, inflow)
        return out, rms[0, 0]

    spread = ("gz", "xy")
    in_specs = (
        P(spread, None, None), P(spread, None, None), P(None, spread, None, None), P(),
        P(None, spread), P(spread), P(spread), P("xy", None),
    )
    return jax.shard_map(
        per_device, mesh=mesh, in_specs=in_specs,
        out_specs=(P(spread, None, None), P()), check_vma=False,
    )
```
